512 devices in a mesh: section: 8 (over y, x_lo), expert: 64 (over x_hi, z, core).
Axes of the slice: x: 4 (x_hi: 2, x_lo: 2; x = x_hi * 2 + x_lo), y: 4, z: 16, core: 2. Of those that a mesh axis runs over, the one named last changes fastest.
Arguments:
- tokens: bfloat16 [8192, 3584], P('expert'), may hold values from -6 to 6
- norm_gain: bfloat16 [3584], replicated, may hold values from 0.25 to 1.75
- router: bfloat16 [3584, 64], replicated, may hold values from -0.09375 to 0.09375
- w_gate: bfloat16 [64, 3584, 1024], P('expert', None, 'section'), may hold values from -0.09375 to 0.09375
- w_up: bfloat16 [64, 3584, 1024], P('expert', None, 'section'), may hold values from -0.09375 to 0.09375
- w_down: bfloat16 [64, 1024, 3584], P('expert', 'section'), may hold values from -0.1875 to 0.1875
- expert_ids: int32 [8192, 3], P('expert'), may hold values from 0 to 63, all different within a row; in each aligned block of 128 rows (0 to 127, 128 to 255, ...) at most 9 rows name the same one
Outputs:
- layer_out: bfloat16 [8192, 3584], P('expert', 'section')
The draws below stay inside these ranges and needn't reach their ends.
Inputs may be any that keep to these rules, and one draw needn't show every extreme that they name: `expert_ids`: each row names 3 different experts. Within each aligned block of 128 rows (the rows of one index of the expert axis) no expert is named by more than 9 rows, and in every draw some expert is named by exactly 9 rows of some block.
All inputs are finite; a program needn't handle non-finite values.
Results may differ from the reference program's by a relative error of at most 0.013.
Values may be sent and summed in bfloat16 or wider, within the bound.
A program may use at most 64 MiB of HBM per device.

```python
import math
import jax
import jax.numpy as jnp
import numpy as np
from jax import lax

D = 3584
FF = 1024
TOP = 3
TOK_DEV = 128
EXPERTS = 64
TOKENS = 8192
CAP = 9
N_SECTION = 8
N_EXPERT = 64


def levels(key, dims, pieces, smallest, top_value):
    loudness = 1.0
    for axis_at, parts in pieces:
        heights = jax.random.uniform(jax.random.fold_in(jax.random.fold_in(key, 6), axis_at), (parts,), jnp.float32, smallest / len(pieces), top_value / len(pieces))
        loudness = loudness * jnp.repeat(jnp.exp(heights), dims[axis_at] // parts).reshape((-1,) + (1,) * (len(dims) - 1 - axis_at))
    return loudness


def assign_block(key, own, number, rows, count, top, reach, skew):
    order = jax.random.permutation(key, count)
    heavy_load, ordinary = shares(count, rows * top, reach, skew, True), shares(count, rows * top, reach, skew, False)
    places = jnp.arange(count)

    def named(sizes, offset_by):
        used = int((sizes > 0).sum())
        fixed = max(1, used // 4)
        shifted = fixed + (places - fixed + offset_by * (used - fixed)) % max(1, count - fixed)
        return jnp.zeros((count,), jnp.int32).at[order[jnp.where(places < fixed, places, shifted)]].set(jnp.asarray(sizes, jnp.int32))

    sizes = jnp.where(number % 4 == 0, named(heavy_load, number // 4), named(ordinary, number - number // 4 - 1))
    mixed = jax.random.permutation(jax.random.fold_in(own, 3), count)
    giver, sink = mixed[0:count // 2 * 2:2], mixed[1:count // 2 * 2:2]
    room = jnp.minimum(sizes[giver] - 1, reach - sizes[sink]) // 2
    room = jnp.where((giver == order[0]) | (sink == order[0]) | (sizes[sink] == 0), 0, jnp.maximum(room, 0))
    shifted = jax.random.randint(jax.random.fold_in(own, 4), (count // 2,), 0, 1 << 20) % (room + 1)
    sizes = sizes.at[giver].add(-shifted).at[sink].add(shifted)
    members = jnp.searchsorted(jnp.cumsum(sizes), jnp.arange(rows * top), side="right").astype(jnp.int32)
    grid = members.reshape(top, rows).T
    grid = grid[jax.random.permutation(jax.random.fold_in(own, 1), rows)]
    offset_by = jax.random.randint(jax.random.fold_in(own, 2), (rows, 1), 0, top)
    return jnp.take_along_axis(grid, (jnp.arange(top)[None, :] + offset_by) % top, axis=1)


def shares(number_of, total, reach, skew, full):
    loads = [(1 << 20) // math.isqrt(standing ** skew) + 1 for standing in range(1, number_of + 1)]
    largest = reach if full else min(reach, max(-(-total // number_of), total * loads[0] // sum(loads)))
    least = 1 if total - largest >= number_of - 1 else 0
    given, spare = [largest] + [least] * (number_of - 1), total - largest - least * (number_of - 1)
    while spare > 0:
        movable = [i for i in range(1, number_of) if given[i] < largest] or [i for i in range(1, number_of) if given[i] < reach]
        pool, remaining = sum([loads[i] for i in movable]), spare
        for i in movable:
            addition = min(reach - given[i], max(1, remaining * loads[i] // pool), spare)
            given[i] = given[i] + addition
            spare = spare - addition
    return np.array(given)


def centred(own_key, dims, width, limit, pieces=(), held_as=jnp.bfloat16):
    factor_of = levels(own_key, dims, pieces, -0.22, 0.18) if pieces else 1.0
    values = jax.random.normal(own_key, dims, jnp.float32) * width * factor_of
    return jnp.minimum(jnp.maximum(values, -limit), limit).astype(held_as)


def setup_inputs(seed: int = 0) -> dict:
    streams_of = jax.random.split(jax.random.key(seed), 8)
    tokens = centred(streams_of[0], (TOKENS, D), 1.0, 6.0, ((0, 64),))
    norm_gain = jnp.clip(1.0 + 0.15 * jax.random.normal(streams_of[1], (D,), jnp.float32), 0.25, 1.75).astype(jnp.bfloat16)
    router = centred(streams_of[2], (D, EXPERTS), D ** -0.5, 0.09375)
    w_gate = centred(streams_of[3], (EXPERTS, D, FF), D ** -0.5, 0.09375, ((0, 64), (2, 8)))
    w_up = centred(streams_of[4], (EXPERTS, D, FF), D ** -0.5, 0.09375, ((0, 64), (2, 8)))
    w_down = centred(streams_of[5], (EXPERTS, FF, D), FF ** -0.5, 0.1875, ((0, 64), (1, 8)))
    expert_ids_keys = jax.random.split(jax.random.fold_in(streams_of[6], 1), TOKENS // TOK_DEV)
    expert_ids_turns = jax.random.permutation(jax.random.fold_in(streams_of[6], 3), TOKENS // TOK_DEV)
    expert_ids = jax.vmap(lambda own, number: assign_block(jax.random.fold_in(streams_of[6], 2), own, number, TOK_DEV, EXPERTS, TOP, CAP, 2))(expert_ids_keys, expert_ids_turns).reshape((TOKENS, TOP))
    return {"tokens": tokens, "norm_gain": norm_gain, "router": router, "w_gate": w_gate, "w_up": w_up, "w_down": w_down, "expert_ids": expert_ids}


EPSILON = 1e-06

def reference(tokens, norm_gain, router, w_gate, w_up, w_down, expert_ids):
    tokens_f = tokens.astype(jnp.float32)
    mean_sq = lax.optimization_barrier(jnp.mean(tokens_f * tokens_f, axis=-1, keepdims=True))
    normed = (tokens_f * lax.rsqrt(mean_sq + EPSILON) * norm_gain.astype(jnp.float32)).astype(jnp.bfloat16)
    logits = jnp.dot(normed, router, preferred_element_type=jnp.float32)
    scores = jax.nn.sigmoid(logits)
    picked = jnp.take_along_axis(scores, expert_ids, axis=1)
    route_weight = 2.5 * picked / lax.optimization_barrier(jnp.sum(picked, axis=1, keepdims=True))
    blocks = N_EXPERT
    tok_block = TOK_DEV
    ids_block = expert_ids.reshape(blocks, tok_block * TOP)
    onehot = (ids_block[:, :, None] == jnp.arange(EXPERTS, dtype=jnp.int32)[None, None, :]).astype(jnp.int32)
    before = jnp.cumsum(onehot, axis=1) - onehot
    slot_rank = lax.optimization_barrier(jnp.sum(onehot * before, axis=-1)).astype(jnp.int32)
    block_ids = jnp.broadcast_to(jnp.arange(blocks, dtype=jnp.int32)[:, None], (blocks, tok_block * TOP))
    row_index = block_ids * tok_block + (jnp.arange(tok_block * TOP, dtype=jnp.int32) // TOP)[None, :]
    row_table = jnp.full((EXPERTS, blocks, CAP), TOKENS, jnp.int32).at[ids_block, block_ids, slot_rank].set(row_index)
    gate_table = jnp.zeros((EXPERTS, blocks, CAP), jnp.float32).at[ids_block, block_ids, slot_rank].set(route_weight.reshape(blocks, tok_block * TOP))
    padded = jnp.concatenate([normed, jnp.zeros((1, D), jnp.bfloat16)], axis=0)
    hid_width = FF // N_SECTION

    def add_expert(totals, expert):
        gather_rows = row_table[expert].reshape(-1)
        inputs = padded[gather_rows]
        gate_act = jnp.dot(inputs, w_gate[expert], preferred_element_type=jnp.float32)
        up_act = jnp.dot(inputs, w_up[expert], preferred_element_type=jnp.float32)
        hidden = (jax.nn.silu(gate_act) * up_act).astype(jnp.bfloat16)
        down = w_down[expert]
        output_sum = jnp.zeros((gather_rows.shape[0], D), jnp.float32)
        for section in range(N_SECTION):
            partial_value = jnp.dot(hidden[:, section * hid_width:(section + 1) * hid_width], down[section * hid_width:(section + 1) * hid_width], preferred_element_type=jnp.float32).astype(jnp.bfloat16)
            output_sum = output_sum + partial_value.astype(jnp.float32)
        weighted = gate_table[expert].reshape(-1)[:, None] * output_sum
        return (totals.at[gather_rows].add(weighted), None)
    totals, _ = lax.scan(add_expert, jnp.zeros((TOKENS + 1, D), jnp.float32), jnp.arange(EXPERTS, dtype=jnp.int32))
    return (tokens_f + totals[:TOKENS]).astype(jnp.bfloat16)
```

```python
import functools

import jax
import jax.numpy as jnp
from jax import lax
from jax.experimental import pallas as pl
from jax.experimental.pallas import tpu as pltpu
from jax.sharding import PartitionSpec as P

EPSILON = 1e-06
MESH = pl.DeviceIdType.MESH
F32 = jnp.float32
BF16 = jnp.bfloat16
LANES = 128
MAIN = 8
Y = 4
CHUNKS = 4


def iota(shape, dim):
    return lax.broadcasted_iota(jnp.int32, shape, dim)


def onehot(mask):
    return jnp.where(mask, 1.0, 0.0).astype(BF16)


def dot(a, b):
    return jnp.dot(a, b, preferred_element_type=F32)


def dot_t(a, b):
    return lax.dot_general(a, b, (((0,), (0,)), ((), ())), preferred_element_type=F32)


def lane_tiles(rows, count, step):
    return jnp.concatenate([rows[j * step : (j + 1) * step] for j in range(count)], axis=1)


def row_tiles(cols, count):
    return jnp.concatenate([cols[:, j * LANES : (j + 1) * LANES] for j in range(count)], axis=0)


def kernel(
    z_size,
    ids_ref,
    tok_ref,
    gain_ref,
    router_ref,
    wg_hbm,
    wu_hbm,
    wd_hbm,
    out_ref,
    dsend,
    xin,
    wgu,
    wdn,
    gown,
    gsend,
    grecv,
    hbuf,
    keep,
    xsend,
    xrecv,
    rsend,
    rrecv,
    csend,
    crecv,
    d_s,
    d_r,
    l_s,
    l_r,
    w_s,
    w_r,
    g_s,
    g_r,
    h_s,
    h_r,
    x_s,
    x_r,
    r_s,
    r_r,
    c_s,
    c_r,
):
    section = lax.axis_index("section")
    expert = lax.axis_index("expert")
    y, x_lo = section // 2, section % 2
    core = expert % 2
    z = (expert // 2) % z_size
    x_hi = expert // (2 * z_size)
    other_core = (core + x_lo) % 2
    peers = dsend.shape[0]
    per_chunk = peers // CHUNKS
    tok_count, width = tok_ref.shape
    part_width = width // Y
    tiles = part_width // LANES
    experts = router_ref.shape[1]

    def peer_expert(i, sign=1):
        half = (i // 2 + 1) // 2
        shift = half * (2 * ((i // 2) % 2) - 1)
        hi = (x_hi + i % 2) % 2
        return (hi * z_size + (z + sign * shift + 2 * z_size) % z_size) * 2 + other_core

    def y_peer(r):
        return ((y + r) % Y) * 2 + x_lo

    x_peer = y * 2 + 1 - x_lo

    def to(section_to, expert_to):
        return {"section": section_to, "expert": expert_to}

    barrier = pltpu.get_barrier_semaphore()

    def greet(i, carry):
        pl.semaphore_signal(
            barrier, inc=1, device_id=to(section, peer_expert(i)), device_id_type=MESH
        )
        return carry

    for r in range(1, Y):
        pl.semaphore_signal(barrier, inc=1, device_id=to(y_peer(r), expert), device_id_type=MESH)
    pl.semaphore_signal(barrier, inc=1, device_id=to(x_peer, expert), device_id_type=MESH)

    @pl.when(x_lo == 1)
    def _():
        greet(0, 0)

    lax.fori_loop(1, peers, greet, 0)

    def rows_of(r):
        return pl.ds(pl.multiple_of(((y + r) % Y) * part_width, LANES), part_width)

    own_weights = [
        pltpu.make_async_copy(wg_hbm.at[0, rows_of(0), :], wgu.at[0, :, 0:LANES], w_r.at[0, 0]),
        pltpu.make_async_copy(
            wu_hbm.at[0, rows_of(0), :], wgu.at[0, :, LANES : 2 * LANES], w_r.at[1, 0]
        ),
        pltpu.make_async_copy(wd_hbm.at[0, :, rows_of(0)], wdn.at[0], w_r.at[2, 0]),
    ]
    for copy in own_weights:
        copy.start()

    square_sum = jnp.zeros((tok_count, LANES), F32)
    for j in range(width // LANES):
        piece = tok_ref[:, j * LANES : (j + 1) * LANES].astype(F32)
        square_sum = square_sum + piece * piece
    mean_sq = jnp.sum(square_sum, axis=1, keepdims=True) / width
    scale = lax.rsqrt(mean_sq + EPSILON)

    columns = pl.ds(pl.multiple_of(y * part_width, LANES), part_width)
    mine = (
        tok_ref[:, columns].astype(F32) * scale * gain_ref[:, columns].astype(F32)
    ).astype(BF16)

    ids = ids_ref[...]
    top = ids.shape[1]
    names = [ids[:, k : k + 1] for k in range(top)]
    expert_lane = iota((tok_count, experts), 1)
    picks = [jnp.where(name == expert_lane, 1.0, 0.0) for name in names]
    chosen = functools.reduce(jnp.add, picks)
    earlier = onehot(iota((tok_count, tok_count), 1) < iota((tok_count, tok_count), 0))
    before = dot(earlier, chosen.astype(BF16))
    slots = [jnp.sum(pick * before, axis=1, keepdims=True).astype(jnp.int32) for pick in picks]

    rows = peers * MAIN
    row_lane = iota((tok_count, rows), 1)
    row_name = peer_expert(row_lane // MAIN)
    row_slot = row_lane % MAIN
    main_of = [onehot((n == row_name) & (s == row_slot)) for n, s in zip(names, slots)]
    main = dot_t(functools.reduce(jnp.add, main_of), mine)
    last_of = [jnp.where((n == row_name) & (s == MAIN), 1.0, 0.0) for n, s in zip(names, slots)]
    last_any = functools.reduce(jnp.add, last_of)
    last = jnp.zeros((rows, LANES), F32)
    for j in range(tiles):
        pick_row = jnp.where(row_slot == j, last_any, 0.0).astype(BF16)
        last = last + dot_t(pick_row, mine[:, j * LANES : (j + 1) * LANES])
    dsend[...] = (
        jnp.concatenate([main, last], axis=1)
        .astype(BF16)
        .reshape(peers, MAIN, part_width + LANES)
    )

    pl.semaphore_wait(barrier, peers - 1 + x_lo + Y)

    def dispatch(i):
        return pltpu.make_async_remote_copy(
            src_ref=dsend.at[i],
            dst_ref=xin.at[0, i],
            send_sem=d_s.at[i],
            recv_sem=d_r.at[i],
            device_id=to(section, peer_expert(i)),
            device_id_type=MESH,
        )

    own_rows = pltpu.make_async_copy(dsend.at[0], xin.at[0, 0], d_r.at[0])

    @pl.when(x_lo == 0)
    def _():
        own_rows.start()

    @pl.when(x_lo == 1)
    def _():
        dispatch(0).start()

    def start_dispatch(i, carry):
        dispatch(i).start()
        return carry

    lax.fori_loop(1, peers, start_dispatch, 0)

    def weight_copies(r):
        there = to(y_peer(r), expert)
        lands = Y - r
        return [
            pltpu.make_async_remote_copy(
                wg_hbm.at[0, rows_of(r), :],
                wgu.at[lands, :, 0:LANES],
                w_s.at[0, r],
                w_r.at[0, lands],
                device_id=there,
                device_id_type=MESH,
            ),
            pltpu.make_async_remote_copy(
                wu_hbm.at[0, rows_of(r), :],
                wgu.at[lands, :, LANES : 2 * LANES],
                w_s.at[1, r],
                w_r.at[1, lands],
                device_id=there,
                device_id_type=MESH,
            ),
            pltpu.make_async_remote_copy(
                wd_hbm.at[0, :, rows_of(r)],
                wdn.at[lands],
                w_s.at[2, r],
                w_r.at[2, lands],
                device_id=there,
                device_id_type=MESH,
            ),
        ]

    weights = {r: weight_copies(r) for r in range(1, Y)}
    for which in range(3):
        for r in (2, 1, 3):
            weights[r][which].start()

    logits = jnp.zeros((tok_count, experts), F32)
    step = width // 7
    for j in range(7):
        cut = slice(j * step, (j + 1) * step)
        normed = (tok_ref[:, cut].astype(F32) * scale * gain_ref[:, cut].astype(F32)).astype(BF16)
        logits = logits + dot(normed, router_ref[cut, :])
    scores = jax.nn.sigmoid(logits)
    picked = [jnp.sum(pick * scores, axis=1, keepdims=True) for pick in picks]
    picked_sum = functools.reduce(jnp.add, picked)
    route = [2.5 * p / picked_sum for p in picked]

    def chunk(q):
        return pl.ds(q * per_chunk, per_chunk)

    def relay(q):
        return pltpu.make_async_remote_copy(
            src_ref=xin.at[0, chunk(q)],
            dst_ref=xin.at[1, chunk(q)],
            send_sem=l_s.at[q],
            recv_sem=l_r.at[q],
            device_id=to(x_peer, expert),
            device_id_type=MESH,
        )

    def wait_dispatch(i, carry):
        dispatch(i).wait_recv()
        return carry

    def stage_relay(q):
        lax.fori_loop(q * per_chunk, (q + 1) * per_chunk, wait_dispatch, 0)
        relay(q).start()

    def gate_copy(q, r):
        return pltpu.make_async_remote_copy(
            src_ref=gsend.at[q, r],
            dst_ref=grecv.at[q, Y - r],
            send_sem=g_s.at[q, r],
            recv_sem=g_r.at[q, Y - r],
            device_id=to(y_peer(r), expert),
            device_id_type=MESH,
        )

    def gate_arrival(q, r):
        return pltpu.make_async_remote_copy(
            src_ref=gsend.at[q, r],
            dst_ref=grecv.at[q, r],
            send_sem=g_s.at[q, r],
            recv_sem=g_r.at[q, r],
            device_id=to(y_peer(r), expert),
            device_id_type=MESH,
        )

    def hidden_copy(q, r):
        return pltpu.make_async_remote_copy(
            src_ref=hbuf.at[q, 0],
            dst_ref=hbuf.at[q, Y - r],
            send_sem=h_s.at[q, r],
            recv_sem=h_r.at[q, Y - r],
            device_id=to(y_peer(r), expert),
            device_id_type=MESH,
        )

    def hidden_arrival(q, r):
        return pltpu.make_async_remote_copy(
            src_ref=hbuf.at[q, 0],
            dst_ref=hbuf.at[q, r],
            send_sem=h_s.at[q, r],
            recv_sem=h_r.at[q, r],
            device_id=to(y_peer(r), expert),
            device_id_type=MESH,
        )

    def pair_copy(q):
        return pltpu.make_async_remote_copy(
            src_ref=xsend.at[q],
            dst_ref=xrecv.at[q],
            send_sem=x_s.at[q],
            recv_sem=x_r.at[q],
            device_id=to(x_peer, expert),
            device_id_type=MESH,
        )

    def returns(i):
        return pltpu.make_async_remote_copy(
            src_ref=rsend.at[i],
            dst_ref=rrecv.at[i],
            send_sem=r_s.at[i],
            recv_sem=r_r.at[i],
            device_id=to(section, peer_expert(i, -1)),
            device_id_type=MESH,
        )

    half_rows = per_chunk * MAIN
    lasts = 2 * per_chunk

    def stage_gate(q):
        relay(q).wait_recv()
        both = jnp.concatenate(
            [
                xin[c, q * per_chunk : (q + 1) * per_chunk].reshape(half_rows, part_width + LANES)
                for c in range(2)
            ],
            axis=0,
        )
        tail = both[:, part_width:]
        at = iota((tiles * lasts, 2 * half_rows), 0)
        pick = onehot(iota((tiles * lasts, 2 * half_rows), 1) == (at % lasts) * MAIN + at // lasts)
        last_rows = lane_tiles(dot(pick, tail), tiles, lasts).astype(BF16)
        inputs = jnp.concatenate([both[:, :part_width], last_rows], axis=0)
        for r in (2, 1, 3):
            gsend[q, r] = dot(inputs, wgu[r]).astype(BF16)
            gate_copy(q, r).start()
        gown[q] = dot(inputs, wgu[0])

    def stage_hidden(q):
        total = gown[q]
        for r in (1, 3, 2):
            gate_arrival(q, r).wait_recv()
            total = total + grecv[q, r].astype(F32)
        gate, up = total[:, :LANES], total[:, LANES:]
        hbuf[q, 0] = (gate / (1.0 + jnp.exp(-gate)) * up).astype(BF16)
        for r in (2, 1, 3):
            hidden_copy(q, r).start()

    def stage_down(q):
        for r in range(1, Y):
            hidden_arrival(q, r).wait_recv()
        hidden = jnp.concatenate([hbuf[q, r] for r in range(Y)], axis=1)
        down = jnp.concatenate([wdn[r] for r in range(Y)], axis=0)
        result = dot(hidden, down)
        last_rows = row_tiles(result[2 * half_rows :], tiles).astype(BF16)
        to_row = iota((2 * half_rows, tiles * lasts), 0)
        at = iota((2 * half_rows, tiles * lasts), 1)
        tail = dot(onehot((at % lasts) * MAIN + at // lasts == to_row), last_rows)
        message = jnp.concatenate([result[: 2 * half_rows], tail], axis=1)
        xsend[q] = message[half_rows:].astype(BF16)
        pair_copy(q).start()
        keep[q] = message[:half_rows]

    def start_return(i, carry):
        returns(i).start()
        return carry

    own_return = pltpu.make_async_copy(rsend.at[0], rrecv.at[0], r_r.at[0])

    def stage_return(q):
        pair_copy(q).wait_recv()
        full = keep[q] + xrecv[q].astype(F32)
        rsend[q * per_chunk : (q + 1) * per_chunk] = full.astype(BF16).reshape(
            per_chunk, MAIN, part_width + LANES
        )
        first = q * per_chunk
        if q == 0:

            @pl.when(x_lo == 0)
            def _():
                own_return.start()

            @pl.when(x_lo == 1)
            def _():
                returns(0).start()

            first = 1
        lax.fori_loop(first, (q + 1) * per_chunk, start_return, 0)

    def wait_weights(kinds):
        for which in kinds:
            own_weights[which].wait()
            for r in (1, 3, 2):
                weights[Y - r][which].wait_recv()

    stages = [stage_relay, stage_gate, stage_hidden, stage_down, stage_return]
    for step_at in range(CHUNKS + len(stages) - 1):
        for number in range(len(stages)):
            q = step_at - number
            if 0 <= q < CHUNKS:
                if number == 1 and q == 0:
                    wait_weights((0, 1))
                if number == 3 and q == 0:
                    wait_weights((2,))
                stages[number](q)

    def wait_return(i, carry):
        returns(i).wait_recv()
        return carry

    lax.fori_loop(0, peers, wait_return, 0)
    back = rrecv[...].reshape(rows, part_width + LANES)
    at = iota((tiles * peers, rows), 0)
    pick = onehot(iota((tiles * peers, rows), 1) == (at % peers) * MAIN + at // peers)
    last_rows = lane_tiles(dot(pick, back[:, part_width:]), tiles, peers).astype(BF16)
    table = jnp.concatenate([back[:, :part_width], last_rows], axis=0)
    peer_name = peer_expert(iota((tok_count, peers), 1))
    mixed = jnp.zeros((tok_count, part_width), F32)
    for k in range(top):
        ninth = onehot((names[k] == peer_name) & (slots[k] == MAIN))
        select = jnp.concatenate([main_of[k], ninth], axis=1)
        mixed = mixed + route[k] * dot(select, table)

    out_width = out_ref.shape[1]
    window = csend.shape[1]
    start_hi = part_width - window

    @pl.when(x_lo == 0)
    def _():
        csend[...] = mixed[:, start_hi:].astype(BF16)

    @pl.when(x_lo == 1)
    def _():
        csend[...] = mixed[:, :window].astype(BF16)

    swap = pltpu.make_async_remote_copy(
        csend, crecv, c_s, c_r, device_id=to(x_peer, expert), device_id_type=MESH
    )
    swap.start()
    swap.wait_recv()

    @pl.when(x_lo == 0)
    def _():
        residual = tok_ref[:, pl.ds(pl.multiple_of(y * part_width, LANES), window)].astype(F32)
        total = residual + (mixed[:, :window] + crecv[...].astype(F32))
        out_ref[...] = total[:, :out_width].astype(BF16)

    @pl.when(x_lo == 1)
    def _():
        residual = tok_ref[
            :, pl.ds(pl.multiple_of(y * part_width + start_hi, LANES), window)
        ].astype(F32)
        total = residual + (mixed[:, start_hi:] + crecv[...].astype(F32))
        out_ref[...] = total[:, window - out_width :].astype(BF16)

    swap.wait_send()

    def wait_sends(i, carry):
        dispatch(i).wait_send()
        returns(i).wait_send()
        return carry

    @pl.when(x_lo == 1)
    def _():
        wait_sends(0, 0)

    lax.fori_loop(1, peers, wait_sends, 0)
    for r in range(1, Y):
        for copy in weights[r]:
            copy.wait_send()
    for q in range(CHUNKS):
        relay(q).wait_send()
        pair_copy(q).wait_send()
        for r in range(1, Y):
            gate_copy(q, r).wait_send()
            hidden_copy(q, r).wait_send()


def per_device(z_size, n_section, tokens, norm_gain, router, w_gate, w_up, w_down, expert_ids):
    tok_count, width = tokens.shape
    part_width = width // Y
    message = part_width + LANES
    peers = 2 * z_size
    per_chunk = peers // CHUNKS
    chunk_rows = 2 * per_chunk * (MAIN + 1)
    half_rows = per_chunk * MAIN
    out_width = width // n_section
    window = -(-out_width // LANES) * LANES
    vmem = pl.BlockSpec(memory_space=pltpu.VMEM)
    hbm = pl.BlockSpec(memory_space=pl.ANY)
    dma = pltpu.SemaphoreType.DMA
    return pl.pallas_call(
        functools.partial(kernel, z_size),
        out_shape=jax.ShapeDtypeStruct((tok_count, out_width), BF16),
        in_specs=[vmem] * 4 + [hbm] * 3,
        out_specs=vmem,
        scratch_shapes=[
            pltpu.VMEM((peers, MAIN, message), BF16),
            pltpu.VMEM((2, peers, MAIN, message), BF16),
            pltpu.VMEM((Y, part_width, 2 * LANES), BF16),
            pltpu.VMEM((Y, LANES, part_width), BF16),
            pltpu.VMEM((CHUNKS, chunk_rows, 2 * LANES), F32),
            pltpu.VMEM((CHUNKS, Y, chunk_rows, 2 * LANES), BF16),
            pltpu.VMEM((CHUNKS, Y, chunk_rows, 2 * LANES), BF16),
            pltpu.VMEM((CHUNKS, Y, chunk_rows, LANES), BF16),
            pltpu.VMEM((CHUNKS, half_rows, message), F32),
            pltpu.VMEM((CHUNKS, half_rows, message), BF16),
            pltpu.VMEM((CHUNKS, half_rows, message), BF16),
            pltpu.VMEM((peers, MAIN, message), BF16),
            pltpu.VMEM((peers, MAIN, message), BF16),
            pltpu.VMEM((tok_count, window), BF16),
            pltpu.VMEM((tok_count, window), BF16),
            dma((peers,)),
            dma((peers,)),
            dma((CHUNKS,)),
            dma((CHUNKS,)),
            dma((3, Y)),
            dma((3, Y)),
            dma((CHUNKS, Y)),
            dma((CHUNKS, Y)),
            dma((CHUNKS, Y)),
            dma((CHUNKS, Y)),
            dma((CHUNKS,)),
            dma((CHUNKS,)),
            dma((peers,)),
            dma((peers,)),
            dma,
            dma,
        ],
        compiler_params=pltpu.CompilerParams(collective_id=0, has_side_effects=True),
    )(expert_ids, tokens, norm_gain.reshape(1, width), router, w_gate, w_up, w_down)


def solution(mesh):
    n_section, n_expert = mesh.shape["section"], mesh.shape["expert"]
    placed = (
        P("expert", None),
        P(),
        P(),
        P("expert", None, "section"),
        P("expert", None, "section"),
        P("expert", "section", None),
        P("expert", None),
    )
    return jax.shard_map(
        functools.partial(per_device, n_expert // 4, n_section),
        mesh=mesh,
        in_specs=placed,
        out_specs=P("expert", "section"),
        check_vma=False,
    )
```
